128 devices in a mesh: tx: 16 (over z, y), ty: 8 (over x, core).
Axes of the slice: x: 4, y: 4, z: 4, core: 2. Of those that a mesh axis runs over, the one named last changes fastest.
Arguments:
- fixed_volume: bfloat16 [256, 256, 128], P('tx', 'ty'), may hold values from -6 to 6
- moving_volume: bfloat16 [256, 256, 128], P('tx', 'ty'), may hold values from -6 to 6
- coarse_motion: float32 [3, 32, 32, 16], P(None, 'tx', 'ty'), may hold values from -4 to 4
- fraction_codes: int32 [3, 32, 32, 16], P(None, 'tx', 'ty'), may hold values from 0 to 7
- block_offsets: int32 [3, 32, 32, 16], P(None, 'tx', 'ty'), may hold values from -8 to 8
Outputs:
- residual: float32 [256, 256, 128], P('tx', 'ty')
- nodal: float32 [3, 32, 32, 16], P(None, 'tx', 'ty')
The draws below stay inside these ranges and needn't reach their ends.
All inputs are finite; a program needn't handle non-finite values.
Results may differ from the reference program's by a relative error of at most 0.0003.
Values may be sent and summed in bfloat16 or wider, within the bound.
A program may use at most 64 MiB of HBM per device.

```python
import jax
import jax.numpy as jnp
from jax import lax

BLOCK = 8
NZ = 128
REACH = 8
BZ = 16
NX = 256
NY = 256
NXB = 32
NYB = 32


def draw_block_offsets(key, part):
    half = REACH // 2
    key_shift, key_field, key_jitter = jax.random.split(jax.random.fold_in(key, 5), 3)
    shift = jax.random.randint(key_shift, (3, 1, 1, 1), -half, half + 1)
    field = jax.random.randint(key_field, (3, NXB // 2, NYB // 2, BZ // 2), -half, half + 1)
    field = jnp.repeat(jnp.repeat(jnp.repeat(field, 2, axis=1), 2, axis=2), 2, axis=3)
    jitter = jax.random.randint(key_jitter, (3, NXB, NYB, BZ), -2, 3)
    total = jnp.clip(shift + field + jitter, -REACH, REACH)
    total = total.at[:, 0, 0, 0].set(REACH)
    total = total.at[:, NXB - 1, NYB - 1, BZ - 1].set(-REACH)
    return total.astype(jnp.int32)


def plant(array, key, low, high):
    index_at = [jax.random.randint(jax.random.fold_in(key, axis), (), 0, length) for axis, length in enumerate(array.shape)]
    main_axis = array.shape.index(max(array.shape))
    neighbour = index_at[:main_axis] + [(index_at[main_axis] + 1) % array.shape[main_axis]] + index_at[main_axis + 1:]
    return array.at[tuple(index_at)].set(low).at[tuple(neighbour)].set(high)


def steps_of(own_key, shape, cuts, smallest, largest):
    loudness, own = 1.0, jax.random.fold_in(own_key, 6)
    for dim, shards_of in cuts:
        draws = jnp.exp(jax.random.uniform(jax.random.fold_in(own, dim), (shards_of,), jnp.float32, smallest / len(cuts), largest / len(cuts)))
        loudness = loudness * jnp.repeat(draws, shape[dim] // shards_of).reshape([-1 if axis == dim else 1 for axis in range(len(shape))])
    return loudness


def normal_values(rng, dims, width, bound, pieces=(), kind=jnp.bfloat16):
    factor_of = steps_of(rng, dims, pieces, -0.22, 0.18) if pieces else 1.0
    values = jax.random.normal(rng, dims, jnp.float32) * width * factor_of
    return jnp.minimum(jnp.maximum(values, -bound), bound).astype(kind)


def setup_inputs(seed: int = 0) -> dict:
    key_list = jax.random.split(jax.random.key(seed), 6)
    return {
        "fixed_volume": normal_values(key_list[0], (NX, NY, NZ), 1.0, 6.0, ((0, 16), (1, 8))),
        "moving_volume": normal_values(key_list[1], (NX, NY, NZ), 1.0, 6.0, ((0, 16), (1, 8))),
        "coarse_motion": normal_values(key_list[2], (3, NXB, NYB, BZ), 0.5, 4.0, ((1, 16), (2, 8)), jnp.float32),
        "fraction_codes": plant(jax.random.randint(key_list[3], (3, NXB, NYB, BZ), 0, BLOCK), jax.random.fold_in(key_list[3], 1), 0, BLOCK - 1).astype(jnp.int32),
        "block_offsets": draw_block_offsets(jax.random.fold_in(key_list[5], 71), 0),
    }


HIGH = lax.Precision.HIGHEST


def taps(code):
    offset_value = (code.astype(jnp.float32) - (BLOCK - 1) / 2.0) / BLOCK
    return jnp.maximum(-offset_value, 0.0), 1.0 - jnp.abs(offset_value), jnp.maximum(offset_value, 0.0)


def prolong_table(cells):
    voxel = jnp.arange(cells, dtype=jnp.int32)
    element = voxel // BLOCK
    weight_low, weight_mid, weight_high = taps(voxel % BLOCK)
    column = jnp.arange(cells // BLOCK + 2, dtype=jnp.int32)
    table = weight_low[:, None] * (column[None, :] == element[:, None]).astype(jnp.float32)
    table = table + weight_mid[:, None] * (column[None, :] == element[:, None] + 1).astype(jnp.float32)
    table = table + weight_high[:, None] * (column[None, :] == element[:, None] + 2).astype(jnp.float32)
    return table


def warp(bricks, codes):
    result = bricks
    for direction in range(3):
        weight_low, weight_mid, weight_high = taps(codes[direction])
        extent = result.shape[direction]
        before_cells = lax.slice_in_dim(result, 0, extent - 2, axis=direction)
        centre_cells = lax.slice_in_dim(result, 1, extent - 1, axis=direction)
        after_cells = lax.slice_in_dim(result, 2, extent, axis=direction)
        result = weight_low * before_cells + weight_mid * centre_cells + weight_high * after_cells
    return result


def gradient(padded):
    grad_x = 0.5 * (padded[2:, 1:-1, 1:-1] - padded[:-2, 1:-1, 1:-1])
    grad_y = 0.5 * (padded[1:-1, 2:, 1:-1] - padded[1:-1, :-2, 1:-1])
    grad_z = 0.5 * (padded[1:-1, 1:-1, 2:] - padded[1:-1, 1:-1, :-2])
    return grad_x, grad_y, grad_z


def prolong(coarse, table_x, table_y, table_z):
    spread = jnp.einsum("xi,cijk->cxjk", table_x, coarse, precision=HIGH)
    spread = jnp.einsum("yj,cxjk->cxyk", table_y, spread, precision=HIGH)
    return jnp.einsum("zk,cxyk->cxyz", table_z, spread, precision=HIGH)


def restrict(fine, table_x, table_y, table_z):
    folded = jnp.einsum("zk,cxyz->cxyk", table_z, fine, precision=HIGH)
    folded = jnp.einsum("yj,cxyk->cxjk", table_y, folded, precision=HIGH)
    return jnp.einsum("xi,cxjk->cijk", table_x, folded, precision=HIGH)


def reference(fixed_volume, moving_volume, coarse_motion, fraction_codes, block_offsets):
    fixed_field = fixed_volume.astype(jnp.float32)
    moving_padded = jnp.pad(moving_volume, REACH + 1)
    brick_edge = BLOCK + 2

    def one_row(row):
        shifts = block_offsets[:, row]
        block_y = jnp.arange(NYB, dtype=jnp.int32)[:, None]
        block_z = jnp.arange(BZ, dtype=jnp.int32)[None, :]
        start_x = (row * BLOCK + shifts[0] + REACH).astype(jnp.int32)
        start_y = (block_y * BLOCK + shifts[1] + REACH).astype(jnp.int32)
        start_z = (block_z * BLOCK + shifts[2] + REACH).astype(jnp.int32)

        def brick(corner_x, corner_y, corner_z):
            return lax.dynamic_slice(moving_padded, (corner_x, corner_y, corner_z), (brick_edge, brick_edge, brick_edge))

        bricks = jax.vmap(brick, out_axes=3)(start_x.reshape(-1), start_y.reshape(-1), start_z.reshape(-1))
        codes = fraction_codes[:, row].reshape(3, -1)
        return warp(bricks.astype(jnp.float32), codes)

    blocks = lax.map(one_row, jnp.arange(NXB, dtype=jnp.int32))
    blocks = blocks.reshape(NXB, BLOCK, BLOCK, BLOCK, NYB, BZ)
    warped = blocks.transpose(0, 1, 4, 2, 5, 3).reshape(NX, NY, NZ)
    grad_x, grad_y, grad_z = gradient(jnp.pad(fixed_field, 1))
    table_x = prolong_table(NX)
    table_y = prolong_table(NY)
    table_z = prolong_table(NZ)
    coarse = jnp.pad(coarse_motion, ((0, 0), (1, 1), (1, 1), (1, 1)))
    motion = prolong(coarse, table_x, table_y, table_z)
    residual = warped + grad_x * motion[0] + grad_y * motion[1] + grad_z * motion[2] - fixed_field
    weighted = jnp.stack([grad_x * residual, grad_y * residual, grad_z * residual])
    nodal = restrict(weighted, table_x, table_y, table_z)[:, 1:-1, 1:-1, 1:-1] / 64.0
    return residual, nodal
```

```python
import functools

import jax
import jax.numpy as jnp
import numpy as np
from jax import lax
from jax.experimental import pallas as pl
from jax.experimental.pallas import tpu as pltpu
from jax.sharding import PartitionSpec as P

MESH = pl.DeviceIdType.MESH
F32 = jnp.float32
BF16 = jnp.bfloat16

DIRS = ((1, 0), (-1, 0), (1, 1), (1, -1), (-1, 1), (-1, -1), (0, 1), (0, -1))
SLOT = {d: k for k, d in enumerate(DIRS)}
FIX_DIRS = ((1, 0), (-1, 0), (0, 1), (0, -1))

EDGE = 9
PLANES = 16 + 2 * EDGE
WIN = 26
ROWS = 40


def hat(values):
    return np.maximum(0.0, 1.0 - np.abs(values))


def ghost_rows():
    return np.array([0, 1, 2, 3, -1, 4, 90, 90])


def constants():
    lane = np.arange(128)
    spread = (np.arange(128)[:, None] == lane[None, :] // 8).astype(np.float32)
    z = np.arange(128)
    along_z = hat((z[:, None] - 3.5) / 8 - np.arange(16)[None, :])
    to_nodes = np.zeros((3, 128, 128), np.float32)
    for c in range(3):
        to_nodes[c, :, 16 * c : 16 * c + 16] = along_z
    from_nodes = np.concatenate([to_nodes[c].T for c in range(3)], axis=1)
    to_nodes = to_nodes.reshape(384, 128)
    x, y = np.arange(16), np.arange(32)
    along_x = hat((x[:, None] - 3.5) / 8 - (np.arange(4)[None, :] - 1))
    along_y = hat((y[:, None] - 3.5) / 8 - ghost_rows()[None, :])
    table = (along_x[:, None, :, None] * along_y[None, :, None, :]).reshape(512, 32)
    table = np.concatenate([table, table, table, np.zeros_like(table)], axis=1)
    fold_y = np.zeros((4, 8, 4, 32), np.float32)
    for i in range(4):
        fold_y[i, :, i, :] = along_y.T
    fold_y = fold_y.reshape(32, 128)
    return [jnp.asarray(a, BF16) for a in (spread, from_nodes, table, fold_y, to_nodes)]


def split(value, parts):
    out = []
    for _ in range(parts - 1):
        piece = value.astype(BF16)
        out.append(piece)
        value = value - piece.astype(F32)
    out.append(value.astype(BF16))
    return out


def dot(a, b):
    return jnp.dot(a, b, preferred_element_type=F32)


def body(
    fixed, moving, coarse, codes, offsets, spread, from_nodes, table, fold_y, to_nodes,
    residual, nodal,
    wide, fixed_wide, fixed_f32, coarse_own, coarse_pack, coarse_in, code_v, offset_v,
    row_v, row_s, quant, quant_wide, spread_v, from_v, table_v, fold_v, to_v,
    hats, windows, known, grads, folded, node_own, node_in,
    local_sem, move_send, move_recv, fix_send, fix_recv, coarse_send, coarse_recv,
    node_send, node_recv,
):
    tx, ty = lax.axis_index("tx"), lax.axis_index("ty")
    count_x, count_y = lax.axis_size("tx"), lax.axis_size("ty")

    def has(dx, dy):
        found = None
        for step, at, count in ((dx, tx, count_x), (dy, ty, count_y)):
            if step:
                test = at > 0 if step < 0 else at < count - 1
                found = test if found is None else jnp.logical_and(found, test)
        return found

    def device(dx, dy):
        return (tx + dx, ty + dy)

    barrier = pltpu.get_barrier_semaphore()
    for d in DIRS:
        @pl.when(has(*d))
        def _(d=d):
            pl.semaphore_signal(barrier, inc=1, device_id=device(*d), device_id_type=MESH)

    local = []
    for k, (src, dst) in enumerate((
        (coarse, coarse_own), (offsets, offset_v), (codes, code_v),
        (moving, wide.at[EDGE : EDGE + 16, 16:48, :]),
        (fixed, fixed_wide.at[1:17, 8:40, :]),
        (spread, spread_v), (from_nodes, from_v), (table, table_v), (fold_y, fold_v), (to_nodes, to_v),
    )):
        copy = pltpu.make_async_copy(src, dst, local_sem.at[k])
        copy.start()
        local.append(copy)

    def span_x(dx, width, base, extent):
        if dx == 1:
            return slice(16 - width, 16), slice(base - width, base)
        if dx == -1:
            return slice(0, width), slice(base + extent, base + extent + width)
        return slice(0, extent), slice(base, base + extent)

    def span_y(dy, width, base):
        if dy == 1:
            return slice(32 - width, 32), slice(base - width, base)
        if dy == -1:
            return slice(0, width), slice(base + 32, base + 32 + width)
        return slice(0, 32), slice(base, base + 32)

    move_copy, move_zone = {}, {}
    for d in DIRS:
        sx, tx_zone = span_x(d[0], EDGE, EDGE, 16)
        sy, ty_zone = span_y(d[1], 16, 16)
        move_zone[d] = (tx_zone, ty_zone)
        k = SLOT[d]
        move_copy[d] = pltpu.make_async_remote_copy(
            src_ref=moving.at[sx, sy, :], dst_ref=wide.at[tx_zone, ty_zone, :],
            send_sem=move_send.at[k], recv_sem=move_recv.at[k],
            device_id=device(*d), device_id_type=MESH,
        )
    fix_copy, fix_zone = {}, {}
    for k, d in enumerate(FIX_DIRS):
        sx, tx_zone = span_x(d[0], 1, 1, 16)
        sy, ty_zone = span_y(d[1], 8, 8)
        fix_zone[d] = (tx_zone, ty_zone)
        fix_copy[d] = pltpu.make_async_remote_copy(
            src_ref=fixed.at[sx, sy, :], dst_ref=fixed_wide.at[tx_zone, ty_zone, :],
            send_sem=fix_send.at[k], recv_sem=fix_recv.at[k],
            device_id=device(*d), device_id_type=MESH,
        )

    def slab(dx):
        return {1: slice(1, 2), -1: slice(0, 1), 0: slice(0, 2)}[dx]

    coarse_copy = {}
    for d in DIRS:
        k = SLOT[d]
        part = slab(d[0])
        coarse_copy[d] = pltpu.make_async_remote_copy(
            src_ref=coarse_pack.at[part], dst_ref=coarse_in.at[k, 0 : part.stop - part.start],
            send_sem=coarse_send.at[k], recv_sem=coarse_recv.at[k],
            device_id=device(*d), device_id_type=MESH,
        )

    local[0].wait()
    coarse_pack[...] = jnp.zeros_like(coarse_pack)
    for c in range(3):
        for X in range(2):
            coarse_pack[X, 0:4, 16 * c : 16 * c + 16] = coarse_own[c, X]

    expected = 0
    for d in DIRS:
        expected = expected + jnp.where(has(*d), 1, 0)
    pl.semaphore_wait(barrier, expected)

    def start(copies, d):
        @pl.when(has(*d))
        def _():
            copies[d].start()

    def arrive(copies, d):
        @pl.when(has(-d[0], -d[1]))
        def _():
            copies[d].wait_recv()

    def absent(d):
        return jnp.logical_not(has(-d[0], -d[1]))

    for d in DIRS[:2]:
        start(coarse_copy, d)
        start(fix_copy, d)
        start(move_copy, d)
    for d in DIRS[2:6]:
        start(coarse_copy, d)
        start(move_copy, d)
    for d in DIRS[6:]:
        start(coarse_copy, d)
        start(fix_copy, d)
        start(move_copy, d)

    for d in DIRS:
        @pl.when(absent(d))
        def _(d=d):
            zx, zy = move_zone[d]
            wide[zx, zy, :] = jnp.zeros((zx.stop - zx.start, zy.stop - zy.start, 128), BF16)
            coarse_in[SLOT[d]] = jnp.zeros((2, 8, 128), F32)
            node_in[SLOT[d]] = jnp.zeros((2, 8, 128), F32)
            if d in fix_zone:
                fx, fy = fix_zone[d]
                fixed_wide[fx, fy, :] = jnp.zeros((fx.stop - fx.start, fy.stop - fy.start, 128), BF16)

    local[1].wait()
    local[2].wait()
    quant[...] = jnp.zeros_like(quant)
    row_v[...] = jnp.zeros_like(row_v)
    for X in range(2):
        late = [jnp.where(code_v[c, X] >= 4, 1, 0) for c in range(3)]
        base_x = offset_v[0, X] + late[0] - 1
        base_y = offset_v[1, X] + late[1] - 1
        column = lax.broadcasted_iota(jnp.int32, (4, 16), 0) + 4 * X
        row_v[4 * X : 4 * X + 4, 0:16] = (
            column * (WIN * ROWS) + (base_x + EDGE) * ROWS + base_y + 16
        )
        step = [(code_v[c, X].astype(F32) - 3.5) * 0.125 for c in range(3)]
        quant[4 * X : 4 * X + 4, 0:16] = offset_v[2, X].astype(F32) + step[2]
        for q in range(2):
            quant[8 + 8 * q + 4 * X : 12 + 8 * q + 4 * X, 0:16] = (
                step[q] + 1.0 - late[q].astype(F32)
            )
    to_scalar = pltpu.make_async_copy(row_v, row_s, local_sem.at[10])
    to_scalar.start()

    local[5].wait()
    quant_wide[...] = dot(quant[...].astype(BF16), spread_v[...])

    lane = lax.broadcasted_iota(jnp.int32, (128, 128), 1).astype(F32)
    depth = lax.broadcasted_iota(jnp.int32, (128, 128), 0).astype(F32)
    gap = depth - lane
    for pair in range(4):
        for side in range(2):
            col = 2 * pair + side
            weights = jnp.maximum(0.0, 1.0 - jnp.abs(gap - quant_wide[col : col + 1, :]))
            hats[pair, :, 128 * side : 128 * side + 128] = weights.astype(BF16)

    def interpolate_z(first, last, group):
        for X in range(2):
            low, high = max(first, 8 * X), min(last, 8 * X + WIN)
            if low >= high:
                continue
            planes = high - low
            rows = wide[low:high, 16 * group : 16 * group + 16, :].reshape(planes * 16, 128)
            for p in range(2):
                at = group - p
                if at < 0 or at > 2:
                    continue
                pair = 2 * X + p
                result = dot(rows, hats[pair]).reshape(planes, 16, 256)
                for side in range(2):
                    begin = 16 * at - 8 * side
                    cut = max(0, -begin)
                    stop = min(16, ROWS - begin)
                    for n in range(planes):
                        to = (2 * pair + side) * WIN * ROWS + (low + n - 8 * X) * ROWS + begin
                        windows[to + cut : to + stop, :] = result[
                            n, cut:stop, 128 * side : 128 * side + 128
                        ]

    local[3].wait()
    own_x = (EDGE, EDGE + 16)
    interpolate_z(*own_x, 1)
    interpolate_z(*own_x, 2)

    for d in DIRS:
        arrive(coarse_copy, d)
    row = lax.broadcasted_iota(jnp.int32, (8, 128), 0)

    def framed(centre, low, high):
        ghost = jnp.where(row == 4, pltpu.roll(low, 1, 0), jnp.where(row == 5, pltpu.roll(high, 5, 0), 0.0))
        return jnp.where(row < 4, centre, ghost)

    nodes = [
        framed(coarse_in[SLOT[1, 0], 0], coarse_in[SLOT[1, 1], 0], coarse_in[SLOT[1, -1], 0]),
        framed(coarse_pack[0], coarse_in[SLOT[0, 1], 0], coarse_in[SLOT[0, -1], 0]),
        framed(coarse_pack[1], coarse_in[SLOT[0, 1], 1], coarse_in[SLOT[0, -1], 1]),
        framed(coarse_in[SLOT[-1, 0], 0], coarse_in[SLOT[-1, 1], 0], coarse_in[SLOT[-1, -1], 0]),
    ]
    local[6].wait()
    nodes = jnp.concatenate(split(jnp.concatenate(nodes, axis=0), 3), axis=0)
    spread_z = dot(nodes, from_v[...])
    spread_z = spread_z[0:32] + spread_z[32:64] + spread_z[64:96]
    pieces = split(spread_z, 3)
    stacked = jnp.concatenate(pieces + [jnp.zeros_like(pieces[0])], axis=0)

    for d in FIX_DIRS:
        arrive(fix_copy, d)
    local[4].wait()
    fixed_f32[...] = fixed_wide[...].astype(F32)
    local[7].wait()
    last_lane = lax.broadcasted_iota(jnp.int32, (32, 128), 1)
    for chunk in range(4):
        motion = dot(table_v[128 * chunk : 128 * chunk + 128, :], stacked)
        for n in range(4):
            at = 4 * chunk + n
            centre = fixed_f32[at + 1, 8:40, :]
            grad_x = 0.5 * (fixed_f32[at + 2, 8:40, :] - fixed_f32[at, 8:40, :])
            grad_y = 0.5 * (fixed_f32[at + 1, 9:41, :] - fixed_f32[at + 1, 7:39, :])
            after = jnp.where(last_lane == 127, 0.0, pltpu.roll(centre, 127, 1))
            before = jnp.where(last_lane == 0, 0.0, pltpu.roll(centre, 1, 1))
            grad_z = 0.5 * (after - before)
            total = -centre
            for c, grad in enumerate((grad_x, grad_y, grad_z)):
                grads[c, at] = grad
                total = total + grad * motion[32 * n : 32 * n + 32, 128 * c : 128 * c + 128]
            known[at] = total

    arrive(move_copy, (0, 1))
    interpolate_z(*own_x, 0)
    arrive(move_copy, (0, -1))
    interpolate_z(*own_x, 3)
    below, above = (0, EDGE), (EDGE + 16, PLANES)
    arrive(move_copy, (1, 0))
    interpolate_z(*below, 1)
    interpolate_z(*below, 2)
    arrive(move_copy, (-1, 0))
    interpolate_z(*above, 1)
    interpolate_z(*above, 2)
    arrive(move_copy, (1, 1))
    interpolate_z(*below, 0)
    arrive(move_copy, (1, -1))
    interpolate_z(*below, 3)
    arrive(move_copy, (-1, 1))
    interpolate_z(*above, 0)
    arrive(move_copy, (-1, -1))
    interpolate_z(*above, 3)
    to_scalar.wait()

    block_of_lane = lax.broadcasted_iota(jnp.int32, (8, 128), 1) // 8
    inner = [1.0 - abs(l - 3.5) / 8 for l in range(8)]
    outer = [abs(l - 3.5) / 8 for l in range(8)]

    def per_row(Y, carry):
        sums = [[None] * 4 for _ in range(3)]
        y8 = pl.multiple_of(8 * Y, 8)

        def add(c, i, value):
            sums[c][i] = value if sums[c][i] is None else sums[c][i] + value

        for X in range(2):
            col = 4 * X + Y
            first, second = [None] * 9, [None] * 9
            for Z in range(16):
                begin = row_s[col, Z]
                mine = block_of_lane == Z
                for n in range(9):
                    a = windows[pl.ds(begin + ROWS * n, 8), :]
                    b = windows[pl.ds(begin + ROWS * n + 1, 8), :]
                    first[n] = a if Z == 0 else jnp.where(mine, a, first[n])
                    second[n] = b if Z == 0 else jnp.where(mine, b, second[n])
            weight_x = jnp.broadcast_to(quant_wide[pl.ds(8 + col, 1), :], (8, 128))
            weight_y = jnp.broadcast_to(quant_wide[pl.ds(16 + col, 1), :], (8, 128))
            lines = [first[n] + weight_y * (second[n] - first[n]) for n in range(9)]
            for l in range(8):
                warped = lines[l] + weight_x * (lines[l + 1] - lines[l])
                at = 8 * X + l
                value = warped + known[at, pl.ds(y8, 8), :]
                residual[at, pl.ds(y8, 8), :] = value
                for c in range(3):
                    term = grads[c, at, pl.ds(y8, 8), :] * value
                    add(c, X + 1, term * inner[l])
                    add(c, X if l < 4 else X + 2, term * outer[l])
        for c in range(3):
            for i in range(4):
                folded[pl.ds(pl.multiple_of(32 * i + y8, 8), 8), 128 * c : 128 * c + 128] = sums[c][i]
        return carry

    lax.fori_loop(0, 4, per_row, 0)

    local[8].wait()
    local[9].wait()
    high, low = split(folded[...], 2)
    rows = dot(fold_v[...], high) + dot(fold_v[...], low)
    high, low = split(rows, 2)
    ends = (dot(high, to_v[...]) + dot(low, to_v[...])) * (1.0 / 64.0)
    node_own[...] = ends.reshape(4, 8, 128)

    node_copy = {}
    for d in DIRS:
        k = SLOT[d]
        part = {1: slice(3, 4), -1: slice(0, 1), 0: slice(1, 3)}[d[0]]
        node_copy[d] = pltpu.make_async_remote_copy(
            src_ref=node_own.at[part], dst_ref=node_in.at[k, 0 : part.stop - part.start],
            send_sem=node_send.at[k], recv_sem=node_recv.at[k],
            device_id=device(*d), device_id_type=MESH,
        )
        start(node_copy, d)
    for d in DIRS:
        arrive(node_copy, d)

    def summed(dy):
        own = [node_own[1], node_own[2]] if dy == 0 else [node_in[SLOT[0, dy], X] for X in range(2)]
        return [own[0] + node_in[SLOT[1, dy], 0], own[1] + node_in[SLOT[-1, dy], 0]]

    centre, from_low, from_high = summed(0), summed(1), summed(-1)
    for X in range(2):
        value = centre[X]
        value = value + jnp.where(row == 0, pltpu.roll(from_low[X], 3, 0), 0.0)
        value = value + jnp.where(row == 3, pltpu.roll(from_high[X], 7, 0), 0.0)
        for c in range(3):
            nodal[c, X] = value[0:4, 16 * c : 16 * c + 16]

    for copies, dirs in ((coarse_copy, DIRS), (fix_copy, FIX_DIRS), (move_copy, DIRS), (node_copy, DIRS)):
        for d in dirs:
            @pl.when(has(*d))
            def _(copies=copies, d=d):
                copies[d].wait_send()


def per_device(fixed_volume, moving_volume, coarse_motion, fraction_codes, block_offsets):
    hbm = pl.BlockSpec(memory_space=pltpu.HBM)
    vmem = pl.BlockSpec(memory_space=pltpu.VMEM)
    dma = pltpu.SemaphoreType.DMA
    return pl.pallas_call(
        body,
        out_shape=(
            jax.ShapeDtypeStruct((16, 32, 128), F32),
            jax.ShapeDtypeStruct((3, 2, 4, 16), F32),
        ),
        in_specs=[hbm] * 10,
        out_specs=(vmem, vmem),
        scratch_shapes=[
            pltpu.VMEM((PLANES, 64, 128), BF16),
            pltpu.VMEM((18, 48, 128), BF16),
            pltpu.VMEM((18, 48, 128), F32),
            pltpu.VMEM((3, 2, 4, 16), F32),
            pltpu.VMEM((2, 8, 128), F32),
            pltpu.VMEM((8, 2, 8, 128), F32),
            pltpu.VMEM((3, 2, 4, 16), jnp.int32),
            pltpu.VMEM((3, 2, 4, 16), jnp.int32),
            pltpu.VMEM((8, 128), jnp.int32),
            pltpu.SMEM((8, 128), jnp.int32),
            pltpu.VMEM((32, 128), F32),
            pltpu.VMEM((32, 128), F32),
            pltpu.VMEM((128, 128), BF16),
            pltpu.VMEM((128, 384), BF16),
            pltpu.VMEM((512, 128), BF16),
            pltpu.VMEM((32, 128), BF16),
            pltpu.VMEM((384, 128), BF16),
            pltpu.VMEM((4, 128, 256), BF16),
            pltpu.VMEM((8 * WIN * ROWS, 128), F32),
            pltpu.VMEM((16, 32, 128), F32),
            pltpu.VMEM((3, 16, 32, 128), F32),
            pltpu.VMEM((128, 384), F32),
            pltpu.VMEM((4, 8, 128), F32),
            pltpu.VMEM((8, 2, 8, 128), F32),
            dma((11,)), dma((8,)), dma((8,)), dma((4,)), dma((4,)), dma((8,)), dma((8,)),
            dma((8,)), dma((8,)),
        ],
        compiler_params=pltpu.CompilerParams(
            collective_id=0, has_side_effects=True, vmem_limit_bytes=32 << 20
        ),
    )(fixed_volume, moving_volume, coarse_motion, fraction_codes, block_offsets, *constants())


def solution(mesh):
    placed = (
        P("tx", "ty", None),
        P("tx", "ty", None),
        P(None, "tx", "ty", None),
        P(None, "tx", "ty", None),
        P(None, "tx", "ty", None),
    )
    return jax.shard_map(
        per_device,
        mesh=mesh,
        in_specs=placed,
        out_specs=(P("tx", "ty", None), P(None, "tx", "ty", None)),
        check_vma=False,
    )
```

```python
import functools

import jax
import jax.numpy as jnp
import numpy as np
from jax import lax
from jax.experimental import pallas as pl
from jax.experimental.pallas import tpu as pltpu
from jax.sharding import PartitionSpec as P

MESH = pl.DeviceIdType.MESH
F32 = jnp.float32
BF16 = jnp.bfloat16

DIRS = ((1, 0), (-1, 0), (1, 1), (1, -1), (-1, 1), (-1, -1), (0, 1), (0, -1))
SLOT = {d: k for k, d in enumerate(DIRS)}
FIX_DIRS = ((1, 0), (-1, 0), (0, 1), (0, -1))

EDGE = 9
PLANES = 16 + 2 * EDGE
WIN = 26
ROWS = 40


def hat(values):
    return np.maximum(0.0, 1.0 - np.abs(values))


def ghost_rows():
    return np.array([0, 1, 2, 3, -1, 4, 90, 90])


def constants():
    lane = np.arange(128)
    spread = (np.arange(128)[:, None] == lane[None, :] // 8).astype(np.float32)
    z = np.arange(128)
    along_z = hat((z[:, None] - 3.5) / 8 - np.arange(16)[None, :])
    to_nodes = np.zeros((3, 128, 128), np.float32)
    for c in range(3):
        to_nodes[c, :, 16 * c : 16 * c + 16] = along_z
    from_nodes = np.concatenate([to_nodes[c].T for c in range(3)], axis=1)
    to_nodes = to_nodes.reshape(384, 128)
    x, y = np.arange(16), np.arange(32)
    along_x = hat((x[:, None] - 3.5) / 8 - (np.arange(4)[None, :] - 1))
    along_y = hat((y[:, None] - 3.5) / 8 - ghost_rows()[None, :])
    table = (along_x[:, None, :, None] * along_y[None, :, None, :]).reshape(512, 32)
    table = np.concatenate([table, table, table, np.zeros_like(table)], axis=1)
    fold_y = np.zeros((4, 8, 4, 32), np.float32)
    for i in range(4):
        fold_y[i, :, i, :] = along_y.T
    fold_y = fold_y.reshape(32, 128)
    return [jnp.asarray(a, BF16) for a in (spread, from_nodes, table, fold_y, to_nodes)]


def split(value, parts):
    out = []
    for _ in range(parts - 1):
        piece = value.astype(BF16)
        out.append(piece)
        value = value - piece.astype(F32)
    out.append(value.astype(BF16))
    return out


def dot(a, b):
    return jnp.dot(a, b, preferred_element_type=F32)


def body(
    fixed, moving, coarse, codes, offsets, spread, from_nodes, table, fold_y, to_nodes,
    residual, nodal,
    wide, fixed_wide, fixed_f32, coarse_own, coarse_pack, coarse_in, code_v, offset_v,
    row_v, row_s, quant, quant_wide, spread_v, from_v, table_v, fold_v, to_v,
    hats, windows, known, grads, folded, node_own, node_in,
    local_sem, move_send, move_recv, fix_send, fix_recv, coarse_send, coarse_recv,
    node_send, node_recv,
):
    tx, ty = lax.axis_index("tx"), lax.axis_index("ty")
    count_x, count_y = lax.axis_size("tx"), lax.axis_size("ty")

    def has(dx, dy):
        found = None
        for step, at, count in ((dx, tx, count_x), (dy, ty, count_y)):
            if step:
                test = at > 0 if step < 0 else at < count - 1
                found = test if found is None else jnp.logical_and(found, test)
        return found

    def device(dx, dy):
        return (tx + dx, ty + dy)

    barrier = pltpu.get_barrier_semaphore()
    for d in DIRS:
        @pl.when(has(*d))
        def _(d=d):
            pl.semaphore_signal(barrier, inc=1, device_id=device(*d), device_id_type=MESH)

    local = []
    for k, (src, dst) in enumerate((
        (coarse, coarse_own), (offsets, offset_v), (codes, code_v),
        (moving, wide.at[EDGE : EDGE + 16, 16:48, :]),
        (fixed, fixed_wide.at[1:17, 8:40, :]),
        (spread, spread_v), (from_nodes, from_v), (table, table_v), (fold_y, fold_v), (to_nodes, to_v),
    )):
        copy = pltpu.make_async_copy(src, dst, local_sem.at[k])
        copy.start()
        local.append(copy)

    def span_x(dx, width, base, extent):
        if dx == 1:
            return slice(16 - width, 16), slice(base - width, base)
        if dx == -1:
            return slice(0, width), slice(base + extent, base + extent + width)
        return slice(0, extent), slice(base, base + extent)

    def span_y(dy, width, base):
        if dy == 1:
            return slice(32 - width, 32), slice(base - width, base)
        if dy == -1:
            return slice(0, width), slice(base + 32, base + 32 + width)
        return slice(0, 32), slice(base, base + 32)

    move_copy, move_zone = {}, {}
    for d in DIRS:
        sx, tx_zone = span_x(d[0], EDGE, EDGE, 16)
        sy, ty_zone = span_y(d[1], 16, 16)
        move_zone[d] = (tx_zone, ty_zone)
        k = SLOT[d]
        move_copy[d] = pltpu.make_async_remote_copy(
            src_ref=moving.at[sx, sy, :], dst_ref=wide.at[tx_zone, ty_zone, :],
            send_sem=move_send.at[k], recv_sem=move_recv.at[k],
            device_id=device(*d), device_id_type=MESH,
        )
    fix_copy, fix_zone = {}, {}
    for k, d in enumerate(FIX_DIRS):
        sx, tx_zone = span_x(d[0], 1, 1, 16)
        sy, ty_zone = span_y(d[1], 8, 8)
        fix_zone[d] = (tx_zone, ty_zone)
        fix_copy[d] = pltpu.make_async_remote_copy(
            src_ref=fixed.at[sx, sy, :], dst_ref=fixed_wide.at[tx_zone, ty_zone, :],
            send_sem=fix_send.at[k], recv_sem=fix_recv.at[k],
            device_id=device(*d), device_id_type=MESH,
        )

    def slab(dx):
        return {1: slice(1, 2), -1: slice(0, 1), 0: slice(0, 2)}[dx]

    coarse_copy = {}
    for d in DIRS:
        k = SLOT[d]
        part = slab(d[0])
        coarse_copy[d] = pltpu.make_async_remote_copy(
            src_ref=coarse_pack.at[part], dst_ref=coarse_in.at[k, 0 : part.stop - part.start],
            send_sem=coarse_send.at[k], recv_sem=coarse_recv.at[k],
            device_id=device(*d), device_id_type=MESH,
        )

    local[0].wait()
    coarse_pack[...] = jnp.zeros_like(coarse_pack)
    for c in range(3):
        for X in range(2):
            coarse_pack[X, 0:4, 16 * c : 16 * c + 16] = coarse_own[c, X]

    expected = 0
    for d in DIRS:
        expected = expected + jnp.where(has(*d), 1, 0)
    pl.semaphore_wait(barrier, expected)

    def start(copies, d):
        @pl.when(has(*d))
        def _():
            copies[d].start()

    def arrive(copies, d):
        @pl.when(has(-d[0], -d[1]))
        def _():
            copies[d].wait_recv()

    def absent(d):
        return jnp.logical_not(has(-d[0], -d[1]))

    for d in DIRS[:2]:
        start(coarse_copy, d)
        start(fix_copy, d)
        start(move_copy, d)
    for d in DIRS[2:6]:
        start(coarse_copy, d)
        start(move_copy, d)
    for d in DIRS[6:]:
        start(coarse_copy, d)
        start(fix_copy, d)
        start(move_copy, d)

    for d in DIRS:
        @pl.when(absent(d))
        def _(d=d):
            zx, zy = move_zone[d]
            wide[zx, zy, :] = jnp.zeros((zx.stop - zx.start, zy.stop - zy.start, 128), BF16)
            coarse_in[SLOT[d]] = jnp.zeros((2, 8, 128), F32)
            node_in[SLOT[d]] = jnp.zeros((2, 8, 128), F32)
            if d in fix_zone:
                fx, fy = fix_zone[d]
                fixed_wide[fx, fy, :] = jnp.zeros((fx.stop - fx.start, fy.stop - fy.start, 128), BF16)

    local[1].wait()
    local[2].wait()
    quant[...] = jnp.zeros_like(quant)
    row_v[...] = jnp.zeros_like(row_v)
    for X in range(2):
        late = [jnp.where(code_v[c, X] >= 4, 1, 0) for c in range(3)]
        base_x = offset_v[0, X] + late[0] - 1
        base_y = offset_v[1, X] + late[1] - 1
        column = lax.broadcasted_iota(jnp.int32, (4, 16), 0) + 4 * X
        row_v[4 * X : 4 * X + 4, 0:16] = (
            column * (WIN * ROWS) + (base_x + EDGE) * ROWS + base_y + 16
        )
        step = [(code_v[c, X].astype(F32) - 3.5) * 0.125 for c in range(3)]
        quant[4 * X : 4 * X + 4, 0:16] = offset_v[2, X].astype(F32) + step[2]
        for q in range(2):
            quant[8 + 8 * q + 4 * X : 12 + 8 * q + 4 * X, 0:16] = (
                step[q] + 1.0 - late[q].astype(F32)
            )
    to_scalar = pltpu.make_async_copy(row_v, row_s, local_sem.at[10])
    to_scalar.start()

    local[5].wait()
    quant_wide[...] = dot(quant[...].astype(BF16), spread_v[...])

    lane = lax.broadcasted_iota(jnp.int32, (128, 128), 1).astype(F32)
    depth = lax.broadcasted_iota(jnp.int32, (128, 128), 0).astype(F32)
    gap = depth - lane
    for pair in range(4):
        for side in range(2):
            col = 2 * pair + side
            weights = jnp.maximum(0.0, 1.0 - jnp.abs(gap - quant_wide[col : col + 1, :]))
            hats[pair, :, 128 * side : 128 * side + 128] = weights.astype(BF16)

    def interpolate_z(first, last, group):
        for X in range(2):
            low, high = max(first, 8 * X), min(last, 8 * X + WIN)
            if low >= high:
                continue
            planes = high - low
            rows = wide[low:high, 16 * group : 16 * group + 16, :].reshape(planes * 16, 128)
            for p in range(2):
                at = group - p
                if at < 0 or at > 2:
                    continue
                pair = 2 * X + p
                result = dot(rows, hats[pair]).reshape(planes, 16, 256)
                for side in range(2):
                    begin = 16 * at - 8 * side
                    cut = max(0, -begin)
                    stop = min(16, ROWS - begin)
                    for n in range(planes):
                        to = (2 * pair + side) * WIN * ROWS + (low + n - 8 * X) * ROWS + begin
                        windows[to + cut : to + stop, :] = result[
                            n, cut:stop, 128 * side : 128 * side + 128
                        ]

    local[3].wait()
    own_x = (EDGE, EDGE + 16)
    interpolate_z(*own_x, 1)
    interpolate_z(*own_x, 2)

    for d in DIRS:
        arrive(coarse_copy, d)
    row = lax.broadcasted_iota(jnp.int32, (8, 128), 0)

    def framed(centre, low, high):
        ghost = jnp.where(row == 4, pltpu.roll(low, 1, 0), jnp.where(row == 5, pltpu.roll(high, 5, 0), 0.0))
        return jnp.where(row < 4, centre, ghost)

    nodes = [
        framed(coarse_in[SLOT[1, 0], 0], coarse_in[SLOT[1, 1], 0], coarse_in[SLOT[1, -1], 0]),
        framed(coarse_pack[0], coarse_in[SLOT[0, 1], 0], coarse_in[SLOT[0, -1], 0]),
        framed(coarse_pack[1], coarse_in[SLOT[0, 1], 1], coarse_in[SLOT[0, -1], 1]),
        framed(coarse_in[SLOT[-1, 0], 0], coarse_in[SLOT[-1, 1], 0], coarse_in[SLOT[-1, -1], 0]),
    ]
    local[6].wait()
    nodes = jnp.concatenate(split(jnp.concatenate(nodes, axis=0), 3), axis=0)
    spread_z = dot(nodes, from_v[...])
    spread_z = spread_z[0:32] + spread_z[32:64] + spread_z[64:96]
    pieces = split(spread_z, 3)
    stacked = jnp.concatenate(pieces + [jnp.zeros_like(pieces[0])], axis=0)

    for d in FIX_DIRS:
        arrive(fix_copy, d)
    local[4].wait()
    fixed_f32[...] = fixed_wide[...].astype(F32)
    local[7].wait()
    last_lane = lax.broadcasted_iota(jnp.int32, (32, 128), 1)
    for chunk in range(4):
        motion = dot(table_v[128 * chunk : 128 * chunk + 128, :], stacked)
        for n in range(4):
            at = 4 * chunk + n
            centre = fixed_f32[at + 1, 8:40, :]
            grad_x = 0.5 * (fixed_f32[at + 2, 8:40, :] - fixed_f32[at, 8:40, :])
            grad_y = 0.5 * (fixed_f32[at + 1, 9:41, :] - fixed_f32[at + 1, 7:39, :])
            after = jnp.where(last_lane == 127, 0.0, pltpu.roll(centre, 127, 1))
            before = jnp.where(last_lane == 0, 0.0, pltpu.roll(centre, 1, 1))
            grad_z = 0.5 * (after - before)
            total = -centre
            for c, grad in enumerate((grad_x, grad_y, grad_z)):
                grads[c, at] = grad
                total = total + grad * motion[32 * n : 32 * n + 32, 128 * c : 128 * c + 128]
            known[at] = total

    arrive(move_copy, (0, 1))
    interpolate_z(*own_x, 0)
    arrive(move_copy, (0, -1))
    interpolate_z(*own_x, 3)
    below, above = (0, EDGE), (EDGE + 16, PLANES)
    arrive(move_copy, (1, 0))
    interpolate_z(*below, 1)
    interpolate_z(*below, 2)
    arrive(move_copy, (-1, 0))
    interpolate_z(*above, 1)
    interpolate_z(*above, 2)
    arrive(move_copy, (1, 1))
    interpolate_z(*below, 0)
    arrive(move_copy, (1, -1))
    interpolate_z(*below, 3)
    arrive(move_copy, (-1, 1))
    interpolate_z(*above, 0)
    arrive(move_copy, (-1, -1))
    interpolate_z(*above, 3)
    to_scalar.wait()

    block_of_lane = lax.broadcasted_iota(jnp.int32, (8, 128), 1) // 8
    inner = [1.0 - abs(l - 3.5) / 8 for l in range(8)]
    outer = [abs(l - 3.5) / 8 for l in range(8)]

    def per_row(Y, carry):
        sums = [[None] * 4 for _ in range(3)]
        y8 = pl.multiple_of(8 * Y, 8)

        def add(c, i, value):
            sums[c][i] = value if sums[c][i] is None else sums[c][i] + value

        for X in range(2):
            col = 4 * X + Y
            first, second = [None] * 9, [None] * 9
            for Z in range(16):
                begin = row_s[col, Z]
                mine = block_of_lane == Z
                for n in range(9):
                    a = windows[pl.ds(begin + ROWS * n, 8), :]
                    b = windows[pl.ds(begin + ROWS * n + 1, 8), :]
                    first[n] = a if Z == 0 else jnp.where(mine, a, first[n])
                    second[n] = b if Z == 0 else jnp.where(mine, b, second[n])
            weight_x = jnp.broadcast_to(quant_wide[pl.ds(8 + col, 1), :], (8, 128))
            weight_y = jnp.broadcast_to(quant_wide[pl.ds(16 + col, 1), :], (8, 128))
            lines = [first[n] + weight_y * (second[n] - first[n]) for n in range(9)]
            for l in range(8):
                warped = lines[l] + weight_x * (lines[l + 1] - lines[l])
                at = 8 * X + l
                value = warped + known[at, pl.ds(y8, 8), :]
                residual[at, pl.ds(y8, 8), :] = value
                for c in range(3):
                    term = grads[c, at, pl.ds(y8, 8), :] * value
                    add(c, X + 1, term * inner[l])
                    add(c, X if l < 4 else X + 2, term * outer[l])
        for c in range(3):
            for i in range(4):
                folded[pl.ds(pl.multiple_of(32 * i + y8, 8), 8), 128 * c : 128 * c + 128] = sums[c][i]
        return carry

    lax.fori_loop(0, 4, per_row, 0)

    local[8].wait()
    local[9].wait()
    high, low = split(folded[...], 2)
    rows = dot(fold_v[...], high) + dot(fold_v[...], low)
    high, low = split(rows, 2)
    ends = (dot(high, to_v[...]) + dot(low, to_v[...])) * (1.0 / 64.0)
    node_own[...] = ends.reshape(4, 8, 128)

    node_copy = {}
    for d in DIRS:
        k = SLOT[d]
        part = {1: slice(3, 4), -1: slice(0, 1), 0: slice(1, 3)}[d[0]]
        node_copy[d] = pltpu.make_async_remote_copy(
            src_ref=node_own.at[part], dst_ref=node_in.at[k, 0 : part.stop - part.start],
            send_sem=node_send.at[k], recv_sem=node_recv.at[k],
            device_id=device(*d), device_id_type=MESH,
        )
        start(node_copy, d)
    for d in DIRS:
        arrive(node_copy, d)

    def summed(dy):
        own = [node_own[1], node_own[2]] if dy == 0 else [node_in[SLOT[0, dy], X] for X in range(2)]
        return [own[0] + node_in[SLOT[1, dy], 0], own[1] + node_in[SLOT[-1, dy], 0]]

    centre, from_low, from_high = summed(0), summed(1), summed(-1)
    for X in range(2):
        value = centre[X]
        value = value + jnp.where(row == 0, pltpu.roll(from_low[X], 3, 0), 0.0)
        value = value + jnp.where(row == 3, pltpu.roll(from_high[X], 7, 0), 0.0)
        for c in range(3):
            nodal[c, X] = value[0:4, 16 * c : 16 * c + 16]

    for copies, dirs in ((coarse_copy, DIRS), (fix_copy, FIX_DIRS), (move_copy, DIRS), (node_copy, DIRS)):
        for d in dirs:
            @pl.when(has(*d))
            def _(copies=copies, d=d):
                copies[d].wait_send()


def write_out(residual, nodal, residual_out, nodal_out, sem):
    copies = [
        pltpu.make_async_copy(residual, residual_out, sem.at[0]),
        pltpu.make_async_copy(nodal, nodal_out, sem.at[1]),
    ]
    for copy in copies:
        copy.start()
    for copy in copies:
        copy.wait()


def per_device(fixed_volume, moving_volume, coarse_motion, fraction_codes, block_offsets):
    hbm = pl.BlockSpec(memory_space=pltpu.HBM)
    vmem = pl.BlockSpec(memory_space=pltpu.VMEM)
    dma = pltpu.SemaphoreType.DMA
    hold = [
        pltpu.with_memory_space_constraint(a, pltpu.HBM)
        for a in (
            fixed_volume, moving_volume, coarse_motion, fraction_codes, block_offsets, *constants()
        )
    ]
    results = pl.pallas_call(
        body,
        out_shape=(
            jax.ShapeDtypeStruct((16, 32, 128), F32),
            jax.ShapeDtypeStruct((3, 2, 4, 16), F32),
        ),
        in_specs=[hbm] * 10,
        out_specs=(vmem, vmem),
        scratch_shapes=[
            pltpu.VMEM((PLANES, 64, 128), BF16),
            pltpu.VMEM((18, 48, 128), BF16),
            pltpu.VMEM((18, 48, 128), F32),
            pltpu.VMEM((3, 2, 4, 16), F32),
            pltpu.VMEM((2, 8, 128), F32),
            pltpu.VMEM((8, 2, 8, 128), F32),
            pltpu.VMEM((3, 2, 4, 16), jnp.int32),
            pltpu.VMEM((3, 2, 4, 16), jnp.int32),
            pltpu.VMEM((8, 128), jnp.int32),
            pltpu.SMEM((8, 128), jnp.int32),
            pltpu.VMEM((32, 128), F32),
            pltpu.VMEM((32, 128), F32),
            pltpu.VMEM((128, 128), BF16),
            pltpu.VMEM((128, 384), BF16),
            pltpu.VMEM((512, 128), BF16),
            pltpu.VMEM((32, 128), BF16),
            pltpu.VMEM((384, 128), BF16),
            pltpu.VMEM((4, 128, 256), BF16),
            pltpu.VMEM((8 * WIN * ROWS, 128), F32),
            pltpu.VMEM((16, 32, 128), F32),
            pltpu.VMEM((3, 16, 32, 128), F32),
            pltpu.VMEM((128, 384), F32),
            pltpu.VMEM((4, 8, 128), F32),
            pltpu.VMEM((8, 2, 8, 128), F32),
            dma((11,)), dma((8,)), dma((8,)), dma((4,)), dma((4,)), dma((8,)), dma((8,)),
            dma((8,)), dma((8,)),
        ],
        compiler_params=pltpu.CompilerParams(
            collective_id=0, has_side_effects=True, vmem_limit_bytes=32 << 20
        ),
    )(*hold)
    return tuple(
        pl.pallas_call(
            write_out,
            out_shape=[jax.ShapeDtypeStruct(r.shape, r.dtype) for r in results],
            in_specs=[vmem, vmem],
            out_specs=[hbm, hbm],
            scratch_shapes=[dma((2,))],
            compiler_params=pltpu.CompilerParams(vmem_limit_bytes=1 << 20),
        )(*results)
    )


def solution(mesh):
    placed = (
        P("tx", "ty", None),
        P("tx", "ty", None),
        P(None, "tx", "ty", None),
        P(None, "tx", "ty", None),
        P(None, "tx", "ty", None),
    )
    return jax.shard_map(
        per_device,
        mesh=mesh,
        in_specs=placed,
        out_specs=(P("tx", "ty", None), P(None, "tx", "ty", None)),
        check_vma=False,
    )
```
